32 devices in a mesh: groups: 2 (over x), tiles: 16 (over z, y, core).
Axes of the slice: x: 2, y: 2, z: 4, core: 2. Of those that a mesh axis runs over, the one named last changes fastest.
Arguments:
- estimate: float32 [768, 16, 512], P(('groups', 'tiles')), parts along dimension 0, may hold values from 0.25 to 4
- observed: bfloat16 [32, 16, 18, 16, 512], P(('groups', 'tiles')), parts along dimension 0, may hold values from 0.25 to 4
- item_tile: int32 [768, 6], P(('groups', 'tiles')), parts along dimension 0, may hold values from 0 to 15, all different within a row; in each aligned block of 24 rows (0 to 23, 24 to 47, ...) at most 18 rows name the same one
- psf_sigma: float32 [6, 3], replicated, may hold values from 0.7 to 3
- view_offsets: int32 [6, 3], replicated, may hold values from -6 to 6
Outputs:
- updated: float32 [768, 16, 512], P(('groups', 'tiles')), parts along dimension 0
The draws below stay inside these ranges and needn't reach their ends.
There are 2 independent parts, one for each index of `groups`. The reference program is written for one: setup_inputs(seed, part) draws one part's arguments, and reference() takes and returns one part's arrays. A program takes and returns all parts, laid end to end along the dimension named above; an argument that names none is the same for every part. Nothing has to cross between parts.
Inputs may be any that keep to these rules, and one draw needn't show every extreme that they name: `item_tile`: the 6 tiles of a row differ; among the 24 rows of one device no tile is named more than 18 times, a bound that some block reaches.
All inputs are finite; a program needn't handle non-finite values.
Results may differ from the reference program's by a relative error of at most 0.0084.
Values may be sent and summed in bfloat16 or wider, within the bound.
No kernel may reach another device: no remote copies, remote signals or barrier semaphores. Data moves between devices by JAX's collectives and lax.ppermute only.
A program may use at most 192 MiB of HBM per device.

```python
import math
import jax
import jax.numpy as jnp
import numpy as np
from jax import lax

BX = 32
BY = 16
BZ = 16
BYX = 512
VIEWS = 6
NB_DEV = 24
NB = 384
MOST = 18
N_TILES = 16


def draw_estimate(key, part):
    wave_count = 6
    key_freq = jax.random.fold_in(key, 11)
    key_phase = jax.random.fold_in(key, 12)
    key_rough = jax.random.fold_in(key, 13)
    freq_x = jax.random.randint(jax.random.fold_in(key_freq, 1), (NB, wave_count), 1, BX // 4 + 1).astype(jnp.float32)
    freq_y = jax.random.randint(jax.random.fold_in(key_freq, 2), (NB, wave_count), 0, BY // 4 + 1).astype(jnp.float32)
    freq_z = jax.random.randint(jax.random.fold_in(key_freq, 3), (NB, wave_count), 0, BZ // 4 + 1).astype(jnp.float32)
    phases = jax.random.uniform(key_phase, (NB, wave_count), jnp.float32, -math.pi, math.pi)
    grid_z = (jnp.arange(BZ, dtype=jnp.float32) / BZ)[None, :, None, None]
    grid_y = (jnp.arange(BY, dtype=jnp.float32) / BY)[None, None, :, None]
    grid_x = (jnp.arange(BX, dtype=jnp.float32) / BX)[None, None, None, :]
    pattern = jnp.zeros((NB, BZ, BY, BX), jnp.float32)
    for which in range(wave_count):
        angles = 2.0 * math.pi * (freq_z[:, which, None, None, None] * grid_z + freq_y[:, which, None, None, None] * grid_y + freq_x[:, which, None, None, None] * grid_x) + phases[:, which, None, None, None]
        pattern = pattern + jnp.cos(angles)
    pattern = pattern / math.sqrt(wave_count / 2.0)
    shaped = 0.95 * jnp.tanh(1.2 * pattern)
    roughness = jax.random.uniform(key_rough, (NB, BZ, BY, BX), jnp.float32, -0.35, 0.35)
    return jnp.exp(shaped + roughness).reshape(NB, BZ, BY * BX)


def set_ends(values, stream_key, least, high):
    longest = values.shape.index(max(values.shape))
    spots = []
    for shift in (0, 1):
        where = [jax.random.randint(jax.random.fold_in(stream_key, axis), (), 0, length) for axis, length in enumerate(values.shape)]
        where[longest] = (where[longest] + shift) % values.shape[longest]
        spots.append(tuple(where))
    return values.at[spots[0]].set(least).at[spots[1]].set(high)


def block_scale(stream_key, dims, pieces, least, largest):
    factor_of, own = 1.0, jax.random.fold_in(stream_key, 6)
    for axis_at, parts in pieces:
        steps = jnp.exp(jax.random.uniform(jax.random.fold_in(own, axis_at), (parts,), jnp.float32, least / len(pieces), largest / len(pieces)))
        factor_of = factor_of * jnp.repeat(steps, dims[axis_at] // parts).reshape([-1 if axis == axis_at else 1 for axis in range(len(dims))])
    return factor_of


def deal_out(own_key, own, number, rows, number_of, top, limit, lean):
    order = jax.random.permutation(own_key, number_of)
    crowded, common = shares(number_of, rows * top, limit, lean, True), shares(number_of, rows * top, limit, lean, False)
    places = jnp.arange(number_of)

    def named(tallies, rotation):
        used = int((tallies > 0).sum())
        fixed = max(1, used // 4)
        shifted = fixed + (places - fixed + rotation * (used - fixed)) % max(1, number_of - fixed)
        return jnp.zeros((number_of,), jnp.int32).at[order[jnp.where(places < fixed, places, shifted)]].set(jnp.asarray(tallies, jnp.int32))

    tallies = jnp.where(number % 4 == 0, named(crowded, number // 4), named(common, number - number // 4 - 1))
    mixed = jax.random.permutation(jax.random.fold_in(own, 3), number_of)
    donor, sink = mixed[0:number_of // 2 * 2:2], mixed[1:number_of // 2 * 2:2]
    slack = jnp.minimum(tallies[donor] - 1, limit - tallies[sink]) // 2
    slack = jnp.where((donor == order[0]) | (sink == order[0]) | (tallies[sink] == 0), 0, jnp.maximum(slack, 0))
    shifted = jax.random.randint(jax.random.fold_in(own, 4), (number_of // 2,), 0, 1 << 20) % (slack + 1)
    tallies = tallies.at[donor].add(-shifted).at[sink].add(shifted)
    labels = jnp.searchsorted(jnp.cumsum(tallies), jnp.arange(rows * top), side="right").astype(jnp.int32)
    grid = labels.reshape(top, rows).T
    grid = grid[jax.random.permutation(jax.random.fold_in(own, 1), rows)]
    rotation = jax.random.randint(jax.random.fold_in(own, 2), (rows, 1), 0, top)
    return jnp.take_along_axis(grid, (jnp.arange(top)[None, :] + rotation) % top, axis=1)


def shares(amount, total, reach, slope, full):
    weights = [(1 << 20) // math.isqrt(rank ** slope) + 1 for rank in range(1, amount + 1)]
    largest = reach if full else min(reach, max(-(-total // amount), total * weights[0] // sum(weights)))
    least = 1 if total - largest >= amount - 1 else 0
    holding, spare = [largest] + [least] * (amount - 1), total - largest - least * (amount - 1)
    while spare > 0:
        movable = [i for i in range(1, amount) if holding[i] < largest] or [i for i in range(1, amount) if holding[i] < reach]
        whole, remaining = sum([weights[i] for i in movable]), spare
        for i in movable:
            more = min(reach - holding[i], max(1, remaining * weights[i] // whole), spare)
            holding[i] = holding[i] + more
            spare = spare - more
    return np.array(holding)


def setup_inputs(seed: int = 0, part: int = 0) -> dict:
    splits = jax.random.split(jax.random.key(seed), 6)
    part_splits = jax.random.split(jax.random.fold_in(splits[5], part), 6)
    estimate = draw_estimate(jax.random.fold_in(jax.random.fold_in(splits[5], part), 71), part)
    observed = jnp.clip(jnp.exp(math.log(4.0) - 2.7725887 * jax.random.uniform(part_splits[1], (N_TILES, N_TILES, MOST, BZ, BYX), jnp.float32) ** block_scale(part_splits[1], (N_TILES, N_TILES, MOST, BZ, BYX), ((0, 16),), -0.2, 0.2)), 0.25, 4.0).astype(jnp.bfloat16)
    item_tile_keys = jax.random.split(jax.random.fold_in(part_splits[2], 1), NB // NB_DEV)
    item_tile_turns = jax.random.permutation(jax.random.fold_in(part_splits[2], 3), NB // NB_DEV)
    item_tile = jax.vmap(lambda own, number: deal_out(jax.random.fold_in(part_splits[2], 2), own, number, NB_DEV, N_TILES, VIEWS, MOST, 2))(item_tile_keys, item_tile_turns).reshape((NB, VIEWS))
    psf_sigma = jnp.clip(jnp.exp(jax.random.uniform(splits[3], (VIEWS, 3), jnp.float32, math.log(0.7), math.log(3.0))), 0.7, 3.0)
    view_offsets = set_ends(jax.random.randint(splits[4], (VIEWS, 3), -6, 7), jax.random.fold_in(splits[4], 1), -6, 6).astype(jnp.int32)
    return dict(estimate=estimate, observed=observed, item_tile=item_tile, psf_sigma=psf_sigma, view_offsets=view_offsets)


tap_reach = 15


def circulant(spread, offset, kernel_length):
    positions = jnp.arange(kernel_length, dtype=jnp.int32)
    distance_raw = positions[None, None, :] - positions[None, :, None] - offset.astype(jnp.int32)[:, None, None]
    half_kernel_length = kernel_length // 2
    distance = jnp.mod(distance_raw + half_kernel_length, kernel_length) - half_kernel_length
    distance_f = distance.astype(jnp.float32)
    kernel_weight = jnp.where(jnp.abs(distance) <= tap_reach, jnp.exp(-distance_f * distance_f / (2.0 * spread[:, None, None] ** 2)), jnp.float32(0.0))
    return (kernel_weight / jnp.sum(kernel_weight, axis=2, keepdims=True)).astype(jnp.bfloat16)


def correct_one(estimate_block, observations, z_matrix, y_matrix, x_matrix):
    section = jnp.einsum('zyk,xk->zyx', estimate_block.astype(jnp.float32), x_matrix.astype(jnp.float32)).astype(jnp.bfloat16)
    section = jnp.einsum('zkx,yk->zyx', section.astype(jnp.float32), y_matrix.astype(jnp.float32)).astype(jnp.bfloat16)
    blurred = jnp.einsum('kyx,zk->zyx', section.astype(jnp.float32), z_matrix.astype(jnp.float32))
    quotient = (observations.astype(jnp.float32) / blurred).astype(jnp.bfloat16)
    section = jnp.einsum('kyx,kz->zyx', quotient.astype(jnp.float32), z_matrix.astype(jnp.float32)).astype(jnp.bfloat16)
    section = jnp.einsum('zkx,ky->zyx', section.astype(jnp.float32), y_matrix.astype(jnp.float32)).astype(jnp.bfloat16)
    return jnp.einsum('zyk,kx->zyx', section.astype(jnp.float32), x_matrix.astype(jnp.float32)).astype(jnp.bfloat16)


def reference(estimate, observed, item_tile, psf_sigma, view_offsets):
    z_table = circulant(psf_sigma[:, 0], view_offsets[:, 0], BZ)
    y_table = circulant(psf_sigma[:, 1], view_offsets[:, 1], BY)
    x_table = circulant(psf_sigma[:, 2], view_offsets[:, 2], BX)
    flat_tiles = item_tile.reshape(N_TILES, NB_DEV * VIEWS)
    hit_table = (flat_tiles[:, :, None] == jnp.arange(N_TILES, dtype=jnp.int32)[None, None, :]).astype(jnp.int32)
    before = jnp.cumsum(hit_table, axis=1) - hit_table
    slot_rank = jnp.sum(before * hit_table, axis=2).astype(jnp.int32).reshape(N_TILES * NB_DEV, VIEWS)
    tile_owners = (jnp.arange(N_TILES * NB_DEV, dtype=jnp.int32) // NB_DEV).astype(jnp.int32)
    est_bf = estimate.astype(jnp.bfloat16).reshape(N_TILES * NB_DEV, BZ, BY, BX)

    def one_block(packed):
        estimate_block, tile_row, rank_row, source = packed
        observations = observed[tile_row, source, rank_row].reshape(VIEWS, BZ, BY, BX)
        copies = jnp.broadcast_to(estimate_block, (VIEWS,) + estimate_block.shape)
        return jax.vmap(correct_one)(copies, observations, z_table, y_table, x_table)

    corrections = lax.map(one_block, (est_bf, item_tile, slot_rank, tile_owners))
    factor = jnp.prod(corrections.astype(jnp.float32), axis=1).reshape(N_TILES * NB_DEV, BZ, BY * BX)
    return estimate * factor
```

```python
import functools

import jax
import jax.numpy as jnp
from jax import lax
from jax.experimental import pallas as pl
from jax.experimental.pallas import tpu as pltpu
from jax.sharding import PartitionSpec as P

BX = 32
BY = 16
TAP_REACH = 15
GROUP = 8
VMEM_LIMIT = 56 << 20


def _table(sigma, offset, n, transposed):
    i = lax.broadcasted_iota(jnp.int32, (n, n), 1 if transposed else 0)
    k = lax.broadcasted_iota(jnp.int32, (n, n), 0 if transposed else 1)
    half = n // 2
    d = ((k - i - offset + half) & (n - 1)) - half
    df = d.astype(jnp.float32)
    w = jnp.where(jnp.abs(d) <= TAP_REACH, jnp.exp(-df * df / (2.0 * sigma * sigma)), 0.0)
    return (w / jnp.sum(w, axis=0 if transposed else 1, keepdims=True)).astype(jnp.bfloat16)


def _expand(table, size, position):
    n = table.shape[0]
    tall = position(lax.broadcasted_iota(jnp.int32, (size, n), 0)) == lax.broadcasted_iota(jnp.int32, (size, n), 1)
    wide = position(lax.broadcasted_iota(jnp.int32, (n, size), 1)) == lax.broadcasted_iota(jnp.int32, (n, size), 0)
    rows = jnp.dot(tall.astype(jnp.bfloat16), table, preferred_element_type=jnp.float32).astype(jnp.bfloat16)
    return jnp.dot(rows, wide.astype(jnp.bfloat16), preferred_element_type=jnp.float32)


def _matrices_kernel(sigma, offset, wf, wb, zf, zb):
    v = pl.program_id(0)
    depth = zf.shape[-1] // GROUP
    for transposed, w_out, z_out in ((True, wf, zb), (False, wb, zf)):
        z_table = _table(sigma[v, 0], offset[v, 0], depth, transposed)
        y_table = _table(sigma[v, 1], offset[v, 1], BY, transposed)
        x_table = _table(sigma[v, 2], offset[v, 2], BX, transposed)
        plane = BY * BX
        w_out[0] = (
            _expand(y_table, plane, lambda r: r // BX) * _expand(x_table, plane, lambda r: r % BX)
        ).astype(jnp.bfloat16)
        size = GROUP * depth
        r = lax.broadcasted_iota(jnp.int32, (size, size), 0) // depth
        c = lax.broadcasted_iota(jnp.int32, (size, size), 1) // depth
        full = _expand(z_table, size, lambda q: q % depth)
        z_out[0] = jnp.where(r == c, full, 0.0).astype(jnp.bfloat16)


def _matrices(sigma, offset, depth, plane):
    views = sigma.shape[0]
    size = GROUP * depth
    smem = pl.BlockSpec(memory_space=pltpu.SMEM)
    return pl.pallas_call(
        _matrices_kernel,
        grid=(views,),
        in_specs=[smem, smem],
        out_specs=[
            pl.BlockSpec((1, plane, plane), lambda v: (v, 0, 0)),
            pl.BlockSpec((1, plane, plane), lambda v: (v, 0, 0)),
            pl.BlockSpec((1, size, size), lambda v: (v, 0, 0)),
            pl.BlockSpec((1, size, size), lambda v: (v, 0, 0)),
        ],
        out_shape=[
            jax.ShapeDtypeStruct((views, plane, plane), jnp.bfloat16),
            jax.ShapeDtypeStruct((views, plane, plane), jnp.bfloat16),
            jax.ShapeDtypeStruct((views, size, size), jnp.bfloat16),
            jax.ShapeDtypeStruct((views, size, size), jnp.bfloat16),
        ],
        compiler_params=pltpu.CompilerParams(vmem_limit_bytes=VMEM_LIMIT),
        name="matrices",
    )(sigma, offset)


def _forward_kernel(est, wf, zf, rb):
    size = zf.shape[-1]
    p2 = jnp.dot(est[...], wf[0], preferred_element_type=jnp.float32).astype(jnp.bfloat16)
    for g in range(est.shape[0] // size):
        rows = slice(g * size, (g + 1) * size)
        rb[0, rows] = 1.0 / jnp.dot(zf[0], p2[rows], preferred_element_type=jnp.float32)


def _forward(est, wf, zf):
    views, plane, _ = wf.shape
    rows, size = est.shape[0], zf.shape[-1]
    return pl.pallas_call(
        _forward_kernel,
        grid=(views,),
        in_specs=[
            pl.BlockSpec((rows, plane), lambda v: (0, 0)),
            pl.BlockSpec((1, plane, plane), lambda v: (v, 0, 0)),
            pl.BlockSpec((1, size, size), lambda v: (v, 0, 0)),
        ],
        out_specs=pl.BlockSpec((1, rows, plane), lambda v: (v, 0, 0)),
        out_shape=jax.ShapeDtypeStruct((views, rows, plane), jnp.float32),
        compiler_params=pltpu.CompilerParams(vmem_limit_bytes=VMEM_LIMIT),
        name="forward",
    )(est, wf, zf)


def _backward_kernel(final, slots, obs, rb, wb, zb, *rest):
    if final:
        est, other, out, acc, q1 = rest
    else:
        out, acc, q1 = rest
    v = pl.program_id(0)
    size = zb.shape[-1]
    depth = obs.shape[1]
    blocks = acc.shape[0] // depth
    for g in range(blocks // GROUP):
        rows = slice(g * size, (g + 1) * size)
        picked = jnp.concatenate(
            [obs[jnp.maximum(slots[v, g * GROUP + j], 0)] for j in range(GROUP)], axis=0
        )
        q = (picked.astype(jnp.float32) * rb[0, rows]).astype(jnp.bfloat16)
        q1[rows] = jnp.dot(zb[0], q, preferred_element_type=jnp.float32).astype(jnp.bfloat16)
    correction = jnp.dot(q1[...], wb[0], preferred_element_type=jnp.float32)

    @pl.when(v == 0)
    def _():
        if final:
            acc[...] = est[...] * other[...].astype(jnp.float32)
        else:
            acc[...] = jnp.ones_like(acc)

    for b in range(blocks):
        rows = slice(b * depth, (b + 1) * depth)
        acc[rows] = acc[rows] * jnp.where(slots[v, b] >= 0, correction[rows], 1.0)

    @pl.when(v == pl.num_programs(0) - 1)
    def _():
        out[...] = acc[...].astype(out.dtype)


def _backward(slots, obs, rb, wb, zb, final=None):
    views, rows, plane = rb.shape
    size, depth = zb.shape[-1], obs.shape[1]
    whole = pl.BlockSpec((rows, plane), lambda v, s: (0, 0))
    return pl.pallas_call(
        functools.partial(_backward_kernel, final is not None),
        grid_spec=pltpu.PrefetchScalarGridSpec(
            num_scalar_prefetch=1,
            grid=(views,),
            in_specs=[
                pl.BlockSpec(obs.shape, lambda v, s: (0, 0, 0)),
                pl.BlockSpec((1, rows, plane), lambda v, s: (v, 0, 0)),
                pl.BlockSpec((1, plane, plane), lambda v, s: (v, 0, 0)),
                pl.BlockSpec((1, size, size), lambda v, s: (v, 0, 0)),
            ]
            + ([whole, whole] if final else []),
            out_specs=whole,
            scratch_shapes=[
                pltpu.VMEM((rows, plane), jnp.float32),
                pltpu.VMEM((rows, plane), jnp.bfloat16),
            ],
        ),
        out_shape=jax.ShapeDtypeStruct((rows, plane), jnp.float32 if final else jnp.bfloat16),
        compiler_params=pltpu.CompilerParams(vmem_limit_bytes=VMEM_LIMIT),
        name="backward_own" if final else "backward_other",
    )(slots, obs, rb, wb, zb, *(final or ()))


def _slots(item_tile, first, count, slot_count):
    blocks, views = item_tile.shape
    flat = item_tile.reshape(-1)
    order = jnp.arange(blocks * views, dtype=jnp.int32)
    before = (flat[:, None] == flat[None, :]) & (order[None, :] < order[:, None])
    rank = jnp.sum(before.astype(jnp.int32), axis=1)
    tile = flat - first
    slot = jnp.where((tile >= 0) & (tile < count), tile * slot_count + rank, -1)
    return slot.reshape(blocks, views).T


def per_device(estimate, observed, item_tile, psf_sigma, view_offsets):
    blocks, depth, plane = estimate.shape
    tiles, slot_count = observed.shape[1:3]
    half = tiles // 2
    mine = lax.axis_index("tiles") // half
    groups = [list(range(half)), list(range(half, tiles))]
    swap = [(t, (t + half) % tiles) for t in range(tiles)]

    by_half = observed[0].reshape(2, half, slot_count, depth, plane)

    def exchange(which):
        sent = lax.dynamic_index_in_dim(by_half, which, 0, keepdims=False)
        got = lax.all_to_all(sent, "tiles", 0, 0, axis_index_groups=groups, tiled=True)
        return got.reshape(half * slot_count, depth, plane)

    est = estimate.reshape(blocks * depth, plane)
    est_bf = est.astype(jnp.bfloat16)
    obs_other = exchange(1 - mine)
    est_other = lax.ppermute(est_bf, "tiles", swap)
    item_tile_other = lax.ppermute(item_tile, "tiles", swap)
    obs_own = exchange(mine)

    wf, wb, zf, zb = _matrices(psf_sigma, view_offsets, depth, plane)
    rb_own = _forward(est_bf, wf, zf)
    rb_other = _forward(est_other, wf, zf)
    slots_own = _slots(item_tile, mine * half, half, slot_count)
    slots_other = _slots(item_tile_other, mine * half, half, slot_count)
    sent_back = _backward(slots_other, obs_other, rb_other, wb, zb)
    product = lax.ppermute(sent_back, "tiles", swap)
    updated = _backward(slots_own, obs_own, rb_own, wb, zb, (est, product))
    return updated.reshape(blocks, depth, plane)


def solution(mesh):
    return jax.shard_map(
        per_device,
        mesh=mesh,
        in_specs=(
            P(("groups", "tiles"), None, None),
            P(("groups", "tiles"), None, None, None, None),
            P(("groups", "tiles"), None),
            P(),
            P(),
        ),
        out_specs=P(("groups", "tiles"), None, None),
        check_vma=False,
    )
```

```python
import functools

import jax
import jax.numpy as jnp
from jax import lax
from jax.experimental import pallas as pl
from jax.experimental.pallas import tpu as pltpu
from jax.sharding import PartitionSpec as P

BX = 32
BY = 16
TAP_REACH = 15
GROUP = 8
VMEM_LIMIT = 28 << 20


def _table(sigma, offset, n, transposed):
    i = lax.broadcasted_iota(jnp.int32, (n, n), 1 if transposed else 0)
    k = lax.broadcasted_iota(jnp.int32, (n, n), 0 if transposed else 1)
    half = n // 2
    d = ((k - i - offset + half) & (n - 1)) - half
    df = d.astype(jnp.float32)
    w = jnp.where(jnp.abs(d) <= TAP_REACH, jnp.exp(-df * df / (2.0 * sigma * sigma)), 0.0)
    return (w / jnp.sum(w, axis=0 if transposed else 1, keepdims=True)).astype(jnp.bfloat16)


def _expand(table, size, position):
    n = table.shape[0]
    tall = position(lax.broadcasted_iota(jnp.int32, (size, n), 0)) == lax.broadcasted_iota(jnp.int32, (size, n), 1)
    wide = position(lax.broadcasted_iota(jnp.int32, (n, size), 1)) == lax.broadcasted_iota(jnp.int32, (n, size), 0)
    rows = jnp.dot(tall.astype(jnp.bfloat16), table, preferred_element_type=jnp.float32).astype(jnp.bfloat16)
    return jnp.dot(rows, wide.astype(jnp.bfloat16), preferred_element_type=jnp.float32)


def _matrices_kernel(sigma, offset, wf, wb, zf, zb):
    v = pl.program_id(0)
    depth = zf.shape[-1] // GROUP
    for transposed, w_out, z_out in ((True, wf, zb), (False, wb, zf)):
        z_table = _table(sigma[v, 0], offset[v, 0], depth, transposed)
        y_table = _table(sigma[v, 1], offset[v, 1], BY, transposed)
        x_table = _table(sigma[v, 2], offset[v, 2], BX, transposed)
        plane = BY * BX
        w_out[0] = (
            _expand(y_table, plane, lambda r: r // BX) * _expand(x_table, plane, lambda r: r % BX)
        ).astype(jnp.bfloat16)
        size = GROUP * depth
        r = lax.broadcasted_iota(jnp.int32, (size, size), 0) // depth
        c = lax.broadcasted_iota(jnp.int32, (size, size), 1) // depth
        full = _expand(z_table, size, lambda q: q % depth)
        z_out[0] = jnp.where(r == c, full, 0.0).astype(jnp.bfloat16)


def _matrices(sigma, offset, depth, plane):
    views = sigma.shape[0]
    size = GROUP * depth
    smem = pl.BlockSpec(memory_space=pltpu.SMEM)
    return pl.pallas_call(
        _matrices_kernel,
        grid=(views,),
        in_specs=[smem, smem],
        out_specs=[
            pl.BlockSpec((1, plane, plane), lambda v: (v, 0, 0)),
            pl.BlockSpec((1, plane, plane), lambda v: (v, 0, 0)),
            pl.BlockSpec((1, size, size), lambda v: (v, 0, 0)),
            pl.BlockSpec((1, size, size), lambda v: (v, 0, 0)),
        ],
        out_shape=[
            pltpu.HBM((views, plane, plane), jnp.bfloat16),
            pltpu.HBM((views, plane, plane), jnp.bfloat16),
            jax.ShapeDtypeStruct((views, size, size), jnp.bfloat16),
            jax.ShapeDtypeStruct((views, size, size), jnp.bfloat16),
        ],
        compiler_params=pltpu.CompilerParams(vmem_limit_bytes=VMEM_LIMIT),
        name="matrices",
    )(sigma, offset)


def _forward_kernel(est, wf, zf, rb):
    size = zf.shape[-1]
    p2 = jnp.dot(est[...], wf[0], preferred_element_type=jnp.float32).astype(jnp.bfloat16)
    for g in range(est.shape[0] // size):
        rows = slice(g * size, (g + 1) * size)
        rb[0, rows] = 1.0 / jnp.dot(zf[0], p2[rows], preferred_element_type=jnp.float32)


def _forward(est, wf, zf):
    views, plane, _ = wf.shape
    rows, size = est.shape[0], zf.shape[-1]
    return pl.pallas_call(
        _forward_kernel,
        grid=(views,),
        in_specs=[
            pl.BlockSpec((rows, plane), lambda v: (0, 0)),
            pl.BlockSpec((1, plane, plane), lambda v: (v, 0, 0)),
            pl.BlockSpec((1, size, size), lambda v: (v, 0, 0)),
        ],
        out_specs=pl.BlockSpec((1, rows, plane), lambda v: (v, 0, 0)),
        out_shape=pltpu.HBM((views, rows, plane), jnp.float32),
        compiler_params=pltpu.CompilerParams(vmem_limit_bytes=VMEM_LIMIT),
        name="forward",
    )(est, wf, zf)


def _fetch(pairs, sems):
    copies = [pltpu.make_async_copy(src, dst, sems.at[n]) for n, (src, dst) in enumerate(pairs)]
    for copy in copies:
        copy.start()
    return copies


def _spans(total, size):
    return [slice(first, first + size) for first in range(0, total, size)]


def _quotient(slots, obs, v, g):
    return jnp.concatenate([obs[jnp.maximum(slots[v, g * GROUP + j], 0)] for j in range(GROUP)], axis=0)


def _multiply_in(slots, v, acc, correction, depth):
    for b, span in enumerate(_spans(acc.shape[0], depth)):
        acc[span] = acc[span] * jnp.where(slots[v, b] >= 0, correction[span], 1.0)


def _places(arrays, buffer, piece=18):
    out, first = [], 0
    for array in arrays:
        for span in _spans(array.shape[0], piece):
            length = min(span.stop, array.shape[0]) - span.start
            out.append((array.at[pl.ds(span.start, length)], buffer.at[pl.ds(first + span.start, length)]))
        first += array.shape[0]
    return out


def _backward_views(slots, obs, rb, wb, zb, q1, acc, arrive_rb, arrive_wb, finish):
    views, rows, size, depth = rb.shape[0], rb.shape[1], zb.shape[-1], obs.shape[1]
    for v in range(views + 1):
        if v < views:
            arrive_rb(v)
        if v > 0:
            arrive_wb(v - 1)
        if v == views:
            finish()
        if v < views:
            for g, span in enumerate(_spans(rows, size)):
                q = (_quotient(slots, obs, v, g).astype(jnp.float32) * rb[v, span]).astype(jnp.bfloat16)
                q1[v, span] = jnp.dot(zb[v], q, preferred_element_type=jnp.float32).astype(jnp.bfloat16)
        if v > 0:
            correction = jnp.dot(q1[v - 1], wb[v - 1], preferred_element_type=jnp.float32)
            _multiply_in(slots, v - 1, acc, correction, depth)


def _other_kernel(n_obs, n_prior, slots, est, zf, zb, *rest):
    prior, rest = rest[:n_prior], rest[n_prior:]
    wf_hbm, wb_hbm = rest[:2]
    obs_hbm, rest = rest[2 : 2 + n_obs], rest[2 + n_obs :]
    out, wf, wb, obs, p2, rb, acc, sems = rest
    views, size = wf.shape[0], zf.shape[-1]
    pairs = [(wf_hbm.at[v], wf.at[v]) for v in range(views)] + _places(obs_hbm, obs)
    last = len(pairs)
    pairs += [(wb_hbm.at[v], wb.at[v]) for v in range(views)]
    copies = _fetch(pairs, sems)
    acc[...] = prior[0][...].astype(jnp.float32) if n_prior else jnp.ones_like(acc)
    for v in range(views + 1):
        if v < views:
            copies[v].wait()
            p2[v] = jnp.dot(est[...], wf[v], preferred_element_type=jnp.float32).astype(jnp.bfloat16)
        if v > 0:
            for span in _spans(rb.shape[1], size):
                rb[v - 1, span] = 1.0 / jnp.dot(zf[v - 1], p2[v - 1, span], preferred_element_type=jnp.float32)
    for copy in copies[views:]:
        copy.wait()
    nothing = lambda *_: None
    _backward_views(slots, obs, rb, wb, zb, p2, acc, nothing, nothing, nothing)
    out[...] = acc[...].astype(out.dtype)


def _own_kernel(n_prior, slots, zb, obs, *rest):
    prior, rest = rest[:n_prior], rest[n_prior:]
    rb_hbm, wb_hbm, est_hbm, acc, rb, wb, est, q1, sems = rest
    views = wb.shape[0]
    pairs = []
    for v in range(views):
        pairs += [(rb_hbm.at[v], rb.at[v]), (wb_hbm.at[v], wb.at[v])]
    copies = _fetch(pairs + [(est_hbm, est)], sems)
    acc[...] = jnp.ones_like(acc)

    def finish():
        copies[-1].wait()
        for factor in (est, *prior):
            acc[...] = acc[...] * factor[...].astype(jnp.float32)

    _backward_views(
        slots, obs, rb, wb, zb, q1, acc, lambda v: copies[2 * v].wait(), lambda v: copies[2 * v + 1].wait(), finish
    )


def _call(kernel, name, out_shape, slots, whole, far, obs, near, scratch):
    count = sum(o.shape[0] for o in obs)
    smem, vmem, hbm = (pl.BlockSpec(memory_space=m) for m in (pltpu.SMEM, pltpu.VMEM, pltpu.HBM))
    fetched = (*far, *obs, *near)
    n_copies = sum(w.shape[0] for w in far) + sum(len(_spans(o.shape[0], 18)) for o in obs) + len(near)
    return pl.pallas_call(
        kernel,
        in_specs=[smem] + [vmem] * len(whole) + [hbm] * len(fetched),
        out_specs=vmem,
        out_shape=out_shape,
        scratch_shapes=[pltpu.VMEM(w.shape, w.dtype) for w in far]
        + [pltpu.VMEM((count, *o.shape[1:]), o.dtype) for o in obs[:1]]
        + [pltpu.VMEM(w.shape, w.dtype) for w in near]
        + scratch
        + [pltpu.SemaphoreType.DMA((n_copies,))],
        compiler_params=pltpu.CompilerParams(vmem_limit_bytes=VMEM_LIMIT),
        name=name,
    )(slots, *whole, *(pltpu.with_memory_space_constraint(x, pltpu.HBM) for x in fetched))


def _other(slots, est, obs, matrices, prior=()):
    wf, wb, zf, zb = matrices
    rows, plane = est.shape
    scratch = [
        pltpu.VMEM((wf.shape[0], rows, plane), jnp.bfloat16),
        pltpu.VMEM((wf.shape[0], rows, plane), jnp.float32),
        pltpu.VMEM((rows, plane), jnp.float32),
    ]
    kernel = functools.partial(_other_kernel, len(obs), len(prior))
    out = pltpu.HBM((rows, plane), jnp.bfloat16)
    return _call(kernel, "other", out, slots, (est, zf, zb, *prior), (wf, wb), obs, (), scratch)


def _own(slots, est, obs, rb, matrices, prior):
    _, wb, _, zb = matrices
    scratch = [pltpu.VMEM(rb.shape, jnp.bfloat16)]
    kernel = functools.partial(_own_kernel, len(prior))
    out = jax.ShapeDtypeStruct(est.shape, jnp.float32)
    whole = [zb] + [pltpu.with_memory_space_constraint(x, pltpu.VMEM) for x in (obs, *prior)]
    return _call(kernel, "own", out, slots, whole, (rb, wb), (), (est,), scratch)


def _slots(item_tile, first, count, slot_count):
    blocks, views = item_tile.shape
    flat = item_tile.reshape(-1)
    order = jnp.arange(blocks * views, dtype=jnp.int32)
    before = (flat[:, None] == flat[None, :]) & (order[None, :] < order[:, None])
    rank = jnp.sum(before.astype(jnp.int32), axis=1)
    tile = flat - first
    slot = jnp.where((tile >= 0) & (tile < count), tile * slot_count + rank, -1)
    return slot.reshape(blocks, views).T


def per_device(estimate, observed, item_tile, psf_sigma, view_offsets):
    blocks, depth, plane = estimate.shape
    tiles, slot_count = observed.shape[1:3]
    half = tiles // 2
    mine = lax.axis_index("tiles") // half
    groups = [list(range(half)), list(range(half, tiles))]
    swap = [(t, (t + half) % tiles) for t in range(tiles)]

    by_half = observed[0].reshape(2, half, slot_count, depth, plane)

    def exchange(sent):
        got = lax.all_to_all(sent, "tiles", 0, 0, axis_index_groups=groups, tiled=True)
        return got.reshape(half * slot_count, depth, plane)

    est = estimate.reshape(blocks * depth, plane)
    est_bf = est.astype(jnp.bfloat16)
    est_other = lax.ppermute(est_bf, "tiles", swap)
    item_tile_other = lax.ppermute(item_tile, "tiles", swap)
    obs_other = exchange(lax.dynamic_index_in_dim(by_half, 1 - mine, 0, keepdims=False))
    matrices = _matrices(psf_sigma, view_offsets, depth, plane)
    rb_own = _forward(est_bf, matrices[0], matrices[2])
    slots_own = _slots(item_tile, mine * half, half, slot_count)
    slots_other = _slots(item_tile_other, mine * half, half, slot_count)
    by_half_2, _ = lax.optimization_barrier((by_half, matrices[2]))
    sent = lax.dynamic_index_in_dim(by_half_2, mine, 0, keepdims=False)
    sent, rb_own, est_other, slots_own, slots_other = lax.optimization_barrier(
        (sent, rb_own, est_other, slots_own, slots_other)
    )
    obs_own = exchange(sent)
    product = lax.ppermute(_other(slots_other, est_other, [obs_other], matrices), "tiles", swap)
    updated = _own(slots_own, est, obs_own, rb_own, matrices, [product])
    return updated.reshape(blocks, depth, plane)


def solution(mesh):
    return jax.shard_map(
        per_device,
        mesh=mesh,
        in_specs=(
            P(("groups", "tiles"), None, None),
            P(("groups", "tiles"), None, None, None, None),
            P(("groups", "tiles"), None),
            P(),
            P(),
        ),
        out_specs=P(("groups", "tiles"), None, None),
        check_vma=False,
    )
```

```python
import functools

import jax
import jax.numpy as jnp
from jax import lax
from jax.experimental import pallas as pl
from jax.experimental.pallas import tpu as pltpu
from jax.sharding import PartitionSpec as P

BX = 32
BY = 16
TAP_REACH = 15
GROUP = 8
VMEM_LIMIT = 28 << 20


def _table(sigma, offset, n, transposed):
    i = lax.broadcasted_iota(jnp.int32, (n, n), 1 if transposed else 0)
    k = lax.broadcasted_iota(jnp.int32, (n, n), 0 if transposed else 1)
    half = n // 2
    d = ((k - i - offset + half) & (n - 1)) - half
    df = d.astype(jnp.float32)
    w = jnp.where(jnp.abs(d) <= TAP_REACH, jnp.exp(-df * df / (2.0 * sigma * sigma)), 0.0)
    return (w / jnp.sum(w, axis=0 if transposed else 1, keepdims=True)).astype(jnp.bfloat16)


def _expand(table, size, position):
    n = table.shape[0]
    tall = position(lax.broadcasted_iota(jnp.int32, (size, n), 0)) == lax.broadcasted_iota(jnp.int32, (size, n), 1)
    wide = position(lax.broadcasted_iota(jnp.int32, (n, size), 1)) == lax.broadcasted_iota(jnp.int32, (n, size), 0)
    rows = jnp.dot(tall.astype(jnp.bfloat16), table, preferred_element_type=jnp.float32).astype(jnp.bfloat16)
    return jnp.dot(rows, wide.astype(jnp.bfloat16), preferred_element_type=jnp.float32)


def _matrices_kernel(sigma, offset, wf, wb, zf, zb):
    v = pl.program_id(0)
    depth = zf.shape[-1] // GROUP
    for transposed, w_out, z_out in ((True, wf, zb), (False, wb, zf)):
        z_table = _table(sigma[v, 0], offset[v, 0], depth, transposed)
        y_table = _table(sigma[v, 1], offset[v, 1], BY, transposed)
        x_table = _table(sigma[v, 2], offset[v, 2], BX, transposed)
        plane = BY * BX
        w_out[0] = (
            _expand(y_table, plane, lambda r: r // BX) * _expand(x_table, plane, lambda r: r % BX)
        ).astype(jnp.bfloat16)
        size = GROUP * depth
        r = lax.broadcasted_iota(jnp.int32, (size, size), 0) // depth
        c = lax.broadcasted_iota(jnp.int32, (size, size), 1) // depth
        full = _expand(z_table, size, lambda q: q % depth)
        z_out[0] = jnp.where(r == c, full, 0.0).astype(jnp.bfloat16)


def _matrices(sigma, offset, depth, plane):
    views = sigma.shape[0]
    size = GROUP * depth
    smem = pl.BlockSpec(memory_space=pltpu.SMEM)
    return pl.pallas_call(
        _matrices_kernel,
        grid=(views,),
        in_specs=[smem, smem],
        out_specs=[
            pl.BlockSpec((1, plane, plane), lambda v: (v, 0, 0)),
            pl.BlockSpec((1, plane, plane), lambda v: (v, 0, 0)),
            pl.BlockSpec((1, size, size), lambda v: (v, 0, 0)),
            pl.BlockSpec((1, size, size), lambda v: (v, 0, 0)),
        ],
        out_shape=[
            pltpu.HBM((views, plane, plane), jnp.bfloat16),
            pltpu.HBM((views, plane, plane), jnp.bfloat16),
            jax.ShapeDtypeStruct((views, size, size), jnp.bfloat16),
            jax.ShapeDtypeStruct((views, size, size), jnp.bfloat16),
        ],
        compiler_params=pltpu.CompilerParams(vmem_limit_bytes=VMEM_LIMIT),
        name="matrices",
    )(sigma, offset)


def _forward_kernel(est, wf, zf, rb):
    size = zf.shape[-1]
    p2 = jnp.dot(est[...], wf[0], preferred_element_type=jnp.float32).astype(jnp.bfloat16)
    for g in range(est.shape[0] // size):
        rows = slice(g * size, (g + 1) * size)
        rb[0, rows] = (1.0 / jnp.dot(zf[0], p2[rows], preferred_element_type=jnp.float32)).astype(rb.dtype)


def _forward(est, wf, zf):
    views, plane, _ = wf.shape
    rows, size = est.shape[0], zf.shape[-1]
    return pl.pallas_call(
        _forward_kernel,
        grid=(views,),
        in_specs=[
            pl.BlockSpec((rows, plane), lambda v: (0, 0)),
            pl.BlockSpec((1, plane, plane), lambda v: (v, 0, 0)),
            pl.BlockSpec((1, size, size), lambda v: (v, 0, 0)),
        ],
        out_specs=pl.BlockSpec((1, rows, plane), lambda v: (v, 0, 0)),
        out_shape=pltpu.HBM((views, rows, plane), jnp.bfloat16),
        compiler_params=pltpu.CompilerParams(vmem_limit_bytes=VMEM_LIMIT),
        name="forward",
    )(est, wf, zf)


def _fetch(pairs, sems):
    copies = [pltpu.make_async_copy(src, dst, sems.at[n]) for n, (src, dst) in enumerate(pairs)]
    for copy in copies:
        copy.start()
    return copies


def _spans(total, size):
    return [slice(first, first + size) for first in range(0, total, size)]


def _quotient(slots, obs, v, g):
    return jnp.concatenate([obs[jnp.maximum(slots[v, g * GROUP + j], 0)] for j in range(GROUP)], axis=0)


def _multiply_in(slots, v, acc, correction, depth):
    for b, span in enumerate(_spans(acc.shape[0], depth)):
        acc[span] = acc[span] * jnp.where(slots[v, b] >= 0, correction[span], 1.0)


def _places(arrays, buffer, piece=18):
    out, first = [], 0
    for array in arrays:
        for span in _spans(array.shape[0], piece):
            length = min(span.stop, array.shape[0]) - span.start
            out.append((array.at[pl.ds(span.start, length)], buffer.at[pl.ds(first + span.start, length)]))
        first += array.shape[0]
    return out


def _backward_views(slots, obs, rb, wb, zb, q1, acc, arrive_rb, arrive_wb, finish):
    views, rows, size, depth = rb.shape[0], rb.shape[1], zb.shape[-1], obs.shape[1]
    for v in range(views + 1):
        if v < views:
            arrive_rb(v)
        if v > 0:
            arrive_wb(v - 1)
        if v == views:
            finish()
        if v < views:
            for g, span in enumerate(_spans(rows, size)):
                q = (_quotient(slots, obs, v, g).astype(jnp.float32) * rb[v, span]).astype(jnp.bfloat16)
                q1[v, span] = jnp.dot(zb[v], q, preferred_element_type=jnp.float32).astype(jnp.bfloat16)
        if v > 0:
            correction = jnp.dot(q1[v - 1], wb[v - 1], preferred_element_type=jnp.float32)
            _multiply_in(slots, v - 1, acc, correction, depth)


def _other_kernel(n_obs, n_prior, slots, est, zf, zb, *rest):
    prior, rest = rest[:n_prior], rest[n_prior:]
    wf_hbm, wb_hbm = rest[:2]
    obs_hbm, rest = rest[2 : 2 + n_obs], rest[2 + n_obs :]
    out, wf, wb, obs, p2, rb, acc, sems = rest
    views, size = wf.shape[0], zf.shape[-1]
    pairs = [(wf_hbm.at[v], wf.at[v]) for v in range(views)] + _places(obs_hbm, obs)
    last = len(pairs)
    pairs += [(wb_hbm.at[v], wb.at[v]) for v in range(views)]
    copies = _fetch(pairs, sems)
    acc[...] = prior[0][...].astype(jnp.float32) if n_prior else jnp.ones_like(acc)
    for v in range(views + 1):
        if v < views:
            copies[v].wait()
            p2[v] = jnp.dot(est[...], wf[v], preferred_element_type=jnp.float32).astype(jnp.bfloat16)
        if v > 0:
            for span in _spans(rb.shape[1], size):
                rb[v - 1, span] = 1.0 / jnp.dot(zf[v - 1], p2[v - 1, span], preferred_element_type=jnp.float32)
    for copy in copies[views:]:
        copy.wait()
    nothing = lambda *_: None
    _backward_views(slots, obs, rb, wb, zb, p2, acc, nothing, nothing, nothing)
    out[...] = acc[...].astype(out.dtype)


def _own_kernel(n_prior, slots, zb, obs, *rest):
    prior, rest = rest[:n_prior], rest[n_prior:]
    rb_hbm, wb_hbm, est_hbm, acc, rb, wb, est, q1, sems = rest
    views = wb.shape[0]
    pairs = []
    for v in range(views):
        pairs += [(rb_hbm.at[v], rb.at[v]), (wb_hbm.at[v], wb.at[v])]
    copies = _fetch(pairs + [(est_hbm, est)], sems)
    acc[...] = prior[0][...].astype(jnp.float32)

    def finish():
        copies[-1].wait()
        acc[...] = acc[...] * est[...]

    _backward_views(
        slots, obs, rb, wb, zb, q1, acc, lambda v: copies[2 * v].wait(), lambda v: copies[2 * v + 1].wait(), finish
    )


def _call(kernel, name, out_shape, slots, whole, far, obs, near, scratch):
    count = sum(o.shape[0] for o in obs)
    smem, vmem, hbm = (pl.BlockSpec(memory_space=m) for m in (pltpu.SMEM, pltpu.VMEM, pltpu.HBM))
    fetched = (*far, *obs, *near)
    n_copies = sum(w.shape[0] for w in far) + sum(len(_spans(o.shape[0], 18)) for o in obs) + len(near)
    return pl.pallas_call(
        kernel,
        in_specs=[smem] + [vmem] * len(whole) + [hbm] * len(fetched),
        out_specs=vmem,
        out_shape=out_shape,
        scratch_shapes=[pltpu.VMEM(w.shape, w.dtype) for w in far]
        + [pltpu.VMEM((count, *o.shape[1:]), o.dtype) for o in obs[:1]]
        + [pltpu.VMEM(w.shape, w.dtype) for w in near]
        + scratch
        + [pltpu.SemaphoreType.DMA((n_copies,))],
        compiler_params=pltpu.CompilerParams(vmem_limit_bytes=VMEM_LIMIT),
        name=name,
    )(slots, *whole, *(pltpu.with_memory_space_constraint(x, pltpu.HBM) for x in fetched))


def _other(slots, est, obs, matrices, prior=()):
    wf, wb, zf, zb = matrices
    rows, plane = est.shape
    scratch = [
        pltpu.VMEM((wf.shape[0], rows, plane), jnp.bfloat16),
        pltpu.VMEM((wf.shape[0], rows, plane), jnp.float32),
        pltpu.VMEM((rows, plane), jnp.float32),
    ]
    kernel = functools.partial(_other_kernel, len(obs), len(prior))
    out = pltpu.HBM((rows, plane), jnp.bfloat16)
    return _call(kernel, "other", out, slots, (est, zf, zb, *prior), (wf, wb), obs, (), scratch)


def _own(slots, est, obs, rb, matrices, prior):
    _, wb, _, zb = matrices
    scratch = [pltpu.VMEM(rb.shape, jnp.bfloat16)]
    kernel = functools.partial(_own_kernel, len(prior))
    out = jax.ShapeDtypeStruct(est.shape, jnp.float32)
    whole = [zb] + [pltpu.with_memory_space_constraint(x, pltpu.VMEM) for x in (obs, *prior)]
    return _call(kernel, "own", out, slots, whole, (rb, wb), (), (est,), scratch)


def _pick_kernel(owners, held, out, buffer, sems_in, sems_out):
    me = lax.axis_index("tiles")
    half = out.shape[0]
    copies = _fetch([(held.at[owners(me, j)], buffer.at[j]) for j in range(half)], sems_in)
    back = []
    for j in range(half):
        copies[j].wait()
        back.append(pltpu.make_async_copy(buffer.at[j], out.at[j], sems_out.at[j]))
        back[j].start()
    for copy in back:
        copy.wait()


def _pick(held, half, owners, name):
    hbm = pl.BlockSpec(memory_space=pltpu.HBM)
    shape = (half, *held.shape[1:])
    return pl.pallas_call(
        functools.partial(_pick_kernel, owners),
        in_specs=[hbm],
        out_specs=hbm,
        out_shape=pltpu.HBM(shape, held.dtype),
        scratch_shapes=[
            pltpu.VMEM(shape, held.dtype),
            pltpu.SemaphoreType.DMA((half,)),
            pltpu.SemaphoreType.DMA((half,)),
        ],
        name=name,
    )(held)


def _slots(item_tile, first, count, slot_count):
    blocks, views = item_tile.shape
    flat = item_tile.reshape(-1)
    order = jnp.arange(blocks * views, dtype=jnp.int32)
    before = (flat[:, None] == flat[None, :]) & (order[None, :] < order[:, None])
    rank = jnp.sum(before.astype(jnp.int32), axis=1)
    tile = flat - first
    slot = jnp.where((tile >= 0) & (tile < count), tile * slot_count + rank, -1)
    return slot.reshape(blocks, views).T


def per_device(estimate, observed, item_tile, psf_sigma, view_offsets):
    blocks, depth, plane = estimate.shape
    tiles, slot_count = observed.shape[1:3]
    half = tiles // 2
    mine = lax.axis_index("tiles") // half
    groups = [list(range(half)), list(range(half, tiles))]
    swap = [(t, (t + half) % tiles) for t in range(tiles)]

    def exchange(sent):
        got = lax.all_to_all(sent, "tiles", 0, 0, axis_index_groups=groups, tiled=True)
        return got.reshape(half * slot_count, depth, plane)

    est = estimate.reshape(blocks * depth, plane)
    est_bf = est.astype(jnp.bfloat16)
    est_other = lax.ppermute(est_bf, "tiles", swap)
    item_tile_other = lax.ppermute(item_tile, "tiles", swap)
    obs_other = exchange(
        _pick(observed[0], half, lambda me, j: (1 - me // half) * half + j, "pick_other")
    )
    matrices = _matrices(psf_sigma, view_offsets, depth, plane)
    rb_own = _forward(est_bf, matrices[0], matrices[2])
    slots_own = _slots(item_tile, mine * half, half, slot_count)
    slots_other = _slots(item_tile_other, mine * half, half, slot_count)
    by_half_2, _ = lax.optimization_barrier((observed[0], matrices[2]))
    sent = _pick(by_half_2, half, lambda me, j: me // half * half + j, "pick_own")
    sent, rb_own, est_other, slots_own, slots_other = lax.optimization_barrier(
        (sent, rb_own, est_other, slots_own, slots_other)
    )
    obs_own = exchange(sent)
    product = lax.ppermute(_other(slots_other, est_other, [obs_other], matrices), "tiles", swap)
    updated = _own(slots_own, est, obs_own, rb_own, matrices, [product])
    return updated.reshape(blocks, depth, plane)


def solution(mesh):
    return jax.shard_map(
        per_device,
        mesh=mesh,
        in_specs=(
            P(("groups", "tiles"), None, None),
            P(("groups", "tiles"), None, None, None, None),
            P(("groups", "tiles"), None),
            P(),
            P(),
        ),
        out_specs=P(("groups", "tiles"), None, None),
        check_vma=False,
    )
```

```python
import functools

import jax
import jax.numpy as jnp
from jax import lax
from jax.experimental import pallas as pl
from jax.experimental.pallas import tpu as pltpu
from jax.sharding import PartitionSpec as P

BX = 32
BY = 16
TAP_REACH = 15
GROUP = 8
VMEM_LIMIT = 28 << 20
OTHER_COST = pl.CostEstimate(flops=30 * 10**9, transcendentals=0, bytes_accessed=100 << 20)


def _table(sigma, offset, n, transposed):
    i = lax.broadcasted_iota(jnp.int32, (n, n), 1 if transposed else 0)
    k = lax.broadcasted_iota(jnp.int32, (n, n), 0 if transposed else 1)
    half = n // 2
    d = ((k - i - offset + half) & (n - 1)) - half
    df = d.astype(jnp.float32)
    w = jnp.where(jnp.abs(d) <= TAP_REACH, jnp.exp(-df * df / (2.0 * sigma * sigma)), 0.0)
    return (w / jnp.sum(w, axis=0 if transposed else 1, keepdims=True)).astype(jnp.bfloat16)


def _expand(table, size, position):
    n = table.shape[0]
    tall = position(lax.broadcasted_iota(jnp.int32, (size, n), 0)) == lax.broadcasted_iota(jnp.int32, (size, n), 1)
    wide = position(lax.broadcasted_iota(jnp.int32, (n, size), 1)) == lax.broadcasted_iota(jnp.int32, (n, size), 0)
    rows = jnp.dot(tall.astype(jnp.bfloat16), table, preferred_element_type=jnp.float32).astype(jnp.bfloat16)
    return jnp.dot(rows, wide.astype(jnp.bfloat16), preferred_element_type=jnp.float32)


def _matrices_kernel(sigma, offset, wf, wb, zf, zb):
    v = pl.program_id(0)
    depth = zf.shape[-1] // GROUP
    for transposed, w_out, z_out in ((True, wf, zb), (False, wb, zf)):
        z_table = _table(sigma[v, 0], offset[v, 0], depth, transposed)
        y_table = _table(sigma[v, 1], offset[v, 1], BY, transposed)
        x_table = _table(sigma[v, 2], offset[v, 2], BX, transposed)
        plane = BY * BX
        w_out[0] = (
            _expand(y_table, plane, lambda r: r // BX) * _expand(x_table, plane, lambda r: r % BX)
        ).astype(jnp.bfloat16)
        size = GROUP * depth
        r = lax.broadcasted_iota(jnp.int32, (size, size), 0) // depth
        c = lax.broadcasted_iota(jnp.int32, (size, size), 1) // depth
        full = _expand(z_table, size, lambda q: q % depth)
        z_out[0] = jnp.where(r == c, full, 0.0).astype(jnp.bfloat16)


def _matrices(sigma, offset, depth, plane):
    views = sigma.shape[0]
    size = GROUP * depth
    smem = pl.BlockSpec(memory_space=pltpu.SMEM)
    return pl.pallas_call(
        _matrices_kernel,
        grid=(views,),
        in_specs=[smem, smem],
        out_specs=[
            pl.BlockSpec((1, plane, plane), lambda v: (v, 0, 0)),
            pl.BlockSpec((1, plane, plane), lambda v: (v, 0, 0)),
            pl.BlockSpec((1, size, size), lambda v: (v, 0, 0)),
            pl.BlockSpec((1, size, size), lambda v: (v, 0, 0)),
        ],
        out_shape=[
            pltpu.HBM((views, plane, plane), jnp.bfloat16),
            pltpu.HBM((views, plane, plane), jnp.bfloat16),
            jax.ShapeDtypeStruct((views, size, size), jnp.bfloat16),
            jax.ShapeDtypeStruct((views, size, size), jnp.bfloat16),
        ],
        compiler_params=pltpu.CompilerParams(vmem_limit_bytes=VMEM_LIMIT),
        name="matrices",
    )(sigma, offset)


def _forward_kernel(est, wf, zf, rb):
    size = zf.shape[-1]
    p2 = jnp.dot(est[...], wf[0], preferred_element_type=jnp.float32).astype(jnp.bfloat16)
    for g in range(est.shape[0] // size):
        rows = slice(g * size, (g + 1) * size)
        rb[0, rows] = (1.0 / jnp.dot(zf[0], p2[rows], preferred_element_type=jnp.float32)).astype(rb.dtype)


def _forward(est, wf, zf):
    views, plane, _ = wf.shape
    rows, size = est.shape[0], zf.shape[-1]
    return pl.pallas_call(
        _forward_kernel,
        grid=(views,),
        in_specs=[
            pl.BlockSpec((rows, plane), lambda v: (0, 0)),
            pl.BlockSpec((1, plane, plane), lambda v: (v, 0, 0)),
            pl.BlockSpec((1, size, size), lambda v: (v, 0, 0)),
        ],
        out_specs=pl.BlockSpec((1, rows, plane), lambda v: (v, 0, 0)),
        out_shape=pltpu.HBM((views, rows, plane), jnp.bfloat16),
        compiler_params=pltpu.CompilerParams(vmem_limit_bytes=VMEM_LIMIT),
        name="forward",
    )(est, wf, zf)


def _fetch(pairs, sems):
    copies = [pltpu.make_async_copy(src, dst, sems.at[n]) for n, (src, dst) in enumerate(pairs)]
    for copy in copies:
        copy.start()
    return copies


def _spans(total, size):
    return [slice(first, first + size) for first in range(0, total, size)]


def _quotient(slots, obs, v, g):
    return jnp.concatenate([obs[jnp.maximum(slots[v, g * GROUP + j], 0)] for j in range(GROUP)], axis=0)


def _multiply_in(slots, v, acc, correction, depth):
    for b, span in enumerate(_spans(acc.shape[0], depth)):
        acc[span] = acc[span] * jnp.where(slots[v, b] >= 0, correction[span], 1.0)


def _places(arrays, buffer, piece=18):
    out, first = [], 0
    for array in arrays:
        for span in _spans(array.shape[0], piece):
            length = min(span.stop, array.shape[0]) - span.start
            out.append((array.at[pl.ds(span.start, length)], buffer.at[pl.ds(first + span.start, length)]))
        first += array.shape[0]
    return out


def _backward_views(slots, obs, rb, wb, zb, q1, acc, arrive_rb, arrive_wb, finish):
    views, rows, size, depth = rb.shape[0], rb.shape[1], zb.shape[-1], obs.shape[1]
    for v in range(views + 1):
        if v < views:
            arrive_rb(v)
        if v > 0:
            arrive_wb(v - 1)
        if v == views:
            finish()
        if v < views:
            for g, span in enumerate(_spans(rows, size)):
                q = (_quotient(slots, obs, v, g).astype(jnp.float32) * rb[v, span]).astype(jnp.bfloat16)
                q1[v, span] = jnp.dot(zb[v], q, preferred_element_type=jnp.float32).astype(jnp.bfloat16)
        if v > 0:
            correction = jnp.dot(q1[v - 1], wb[v - 1], preferred_element_type=jnp.float32)
            _multiply_in(slots, v - 1, acc, correction, depth)


def _other_kernel(n_obs, n_prior, slots, est, zf, zb, *rest):
    prior, rest = rest[:n_prior], rest[n_prior:]
    wf_hbm, wb_hbm = rest[:2]
    obs_hbm, rest = rest[2 : 2 + n_obs], rest[2 + n_obs :]
    out, wf, wb, obs, p2, rb, acc, sems = rest
    views, size = wf.shape[0], zf.shape[-1]
    pairs = [(wf_hbm.at[v], wf.at[v]) for v in range(views)] + _places(obs_hbm, obs)
    last = len(pairs)
    pairs += [(wb_hbm.at[v], wb.at[v]) for v in range(views)]
    copies = _fetch(pairs, sems)
    acc[...] = prior[0][...].astype(jnp.float32) if n_prior else jnp.ones_like(acc)
    for v in range(views + 1):
        if v < views:
            copies[v].wait()
            p2[v] = jnp.dot(est[: rb.shape[1]], wf[v], preferred_element_type=jnp.float32).astype(jnp.bfloat16)
        if v > 0:
            for span in _spans(rb.shape[1], size):
                rb[v - 1, span] = 1.0 / jnp.dot(zf[v - 1], p2[v - 1, span], preferred_element_type=jnp.float32)
    for copy in copies[views:]:
        copy.wait()
    nothing = lambda *_: None
    _backward_views(slots, obs, rb, wb, zb, p2, acc, nothing, nothing, nothing)
    out[...] = acc[...].astype(out.dtype)


def _own_kernel(n_prior, slots, zb, obs, *rest):
    prior, rest = rest[:n_prior], rest[n_prior:]
    rb_hbm, wb_hbm, est_hbm, acc, rb, wb, est, q1, sems = rest
    views = wb.shape[0]
    pairs = []
    for v in range(views):
        pairs += [(rb_hbm.at[v], rb.at[v]), (wb_hbm.at[v], wb.at[v])]
    copies = _fetch(pairs + [(est_hbm, est)], sems)
    acc[...] = prior[0][...].astype(jnp.float32)

    def finish():
        copies[-1].wait()
        acc[...] = acc[...] * est[...]

    _backward_views(
        slots, obs, rb, wb, zb, q1, acc, lambda v: copies[2 * v].wait(), lambda v: copies[2 * v + 1].wait(), finish
    )


def _call(kernel, name, out_shape, slots, whole, far, obs, near, scratch, cost=None):
    count = sum(o.shape[0] for o in obs)
    smem, vmem, hbm = (pl.BlockSpec(memory_space=m) for m in (pltpu.SMEM, pltpu.VMEM, pltpu.HBM))
    fetched = (*far, *obs, *near)
    n_copies = sum(w.shape[0] for w in far) + sum(len(_spans(o.shape[0], 18)) for o in obs) + len(near)
    return pl.pallas_call(
        kernel,
        in_specs=[smem] + [vmem] * len(whole) + [hbm] * len(fetched),
        out_specs=vmem,
        out_shape=out_shape,
        scratch_shapes=[pltpu.VMEM(w.shape, w.dtype) for w in far]
        + [pltpu.VMEM((count, *o.shape[1:]), o.dtype) for o in obs[:1]]
        + [pltpu.VMEM(w.shape, w.dtype) for w in near]
        + scratch
        + [pltpu.SemaphoreType.DMA((n_copies,))],
        compiler_params=pltpu.CompilerParams(vmem_limit_bytes=VMEM_LIMIT),
        cost_estimate=cost,
        name=name,
    )(slots, *whole, *(pltpu.with_memory_space_constraint(x, pltpu.HBM) for x in fetched))


def _other(slots, est, obs, matrices, prior=()):
    wf, wb, zf, zb = matrices
    rows, plane = slots.shape[1] * obs[0].shape[1], est.shape[1]
    scratch = [
        pltpu.VMEM((wf.shape[0], rows, plane), jnp.bfloat16),
        pltpu.VMEM((wf.shape[0], rows, plane), jnp.float32),
        pltpu.VMEM((rows, plane), jnp.float32),
    ]
    kernel = functools.partial(_other_kernel, len(obs), len(prior))
    out = pltpu.HBM((rows, plane), jnp.bfloat16)
    return _call(kernel, "other", out, slots, (est, zf, zb, *prior), (wf, wb), obs, (), scratch, OTHER_COST)


def _own(slots, est, obs, rb, matrices, prior):
    _, wb, _, zb = matrices
    scratch = [pltpu.VMEM(rb.shape, jnp.bfloat16)]
    kernel = functools.partial(_own_kernel, len(prior))
    out = jax.ShapeDtypeStruct(est.shape, jnp.float32)
    whole = [zb] + [pltpu.with_memory_space_constraint(x, pltpu.VMEM) for x in (obs, *prior)]
    return _call(kernel, "own", out, slots, whole, (rb, wb), (), (est,), scratch)


def _pick_kernel(owners, held, *rest):
    *outs, buffer, sems_in, sems_out = rest
    me = lax.axis_index("tiles")
    half = buffer.shape[0]
    copies = _fetch([(held.at[owners(me, j)], buffer.at[j]) for j in range(half)], sems_in)
    back, places = [], [out.at[n] for out in outs for n in range(out.shape[0])]
    for j in range(half):
        copies[j].wait()
        back.append(pltpu.make_async_copy(buffer.at[j], places[j], sems_out.at[j]))
        back[j].start()
    for copy in back:
        copy.wait()


def _pick(held, counts, owners, name):
    hbm = pl.BlockSpec(memory_space=pltpu.HBM)
    half = sum(counts)
    return pl.pallas_call(
        functools.partial(_pick_kernel, owners),
        in_specs=[hbm],
        out_specs=[hbm] * len(counts),
        out_shape=[pltpu.HBM((count, *held.shape[1:]), held.dtype) for count in counts],
        scratch_shapes=[
            pltpu.VMEM((half, *held.shape[1:]), held.dtype),
            pltpu.SemaphoreType.DMA((half,)),
            pltpu.SemaphoreType.DMA((half,)),
        ],
        name=name,
    )(held)


def _slots(item_tile, first, count, slot_count, place=lambda tile: tile):
    blocks, views = item_tile.shape
    flat = item_tile.reshape(-1)
    order = jnp.arange(blocks * views, dtype=jnp.int32)
    before = (flat[:, None] == flat[None, :]) & (order[None, :] < order[:, None])
    rank = jnp.sum(before.astype(jnp.int32), axis=1)
    tile = flat - first
    slot = jnp.where((tile >= 0) & (tile < count), place(tile) * slot_count + rank, -1)
    return slot.reshape(blocks, views).T


def per_device(estimate, observed, item_tile, psf_sigma, view_offsets):
    blocks, depth, plane = estimate.shape
    tiles, slot_count = observed.shape[1:3]
    views = item_tile.shape[1]
    half, quarter = tiles // 2, tiles // 4
    me = lax.axis_index("tiles")
    mine, side, turn = me // half, me // quarter % 2, me % quarter
    halves = [list(range(first, first + half)) for first in range(0, tiles, half)]
    quarters = [list(range(first, first + quarter)) for first in range(0, tiles, quarter)]
    swap = [(t, (t + half) % tiles) for t in range(tiles)]

    def exchange(sent, groups):
        got = lax.all_to_all(sent, "tiles", 0, 0, axis_index_groups=groups, tiled=True)
        return got.reshape(-1, depth, plane)

    def owner(me, j):
        near = me // quarter % 2 * quarter + j
        across = (1 - me // quarter % 2) * quarter + (me + j) % quarter
        return (1 - me // half) * half + (near if j < quarter else across)

    def place(tile):
        return jnp.where(tile // quarter == side, tile % quarter, quarter + (turn - tile % quarter + quarter) % quarter)

    est = estimate.reshape(blocks * depth, plane)
    est_bf = est.astype(jnp.bfloat16)
    names = item_tile.reshape(-1).astype(jnp.bfloat16)
    names = jnp.pad(names, (0, depth * plane - names.shape[0])).reshape(depth, plane)
    est_other = lax.ppermute(jnp.concatenate([est_bf, names], axis=0), "tiles", swap)
    near, *across = _pick(observed[0], [quarter] + [1] * quarter, owner, "pick_other")
    obs_near = exchange(near, quarters)
    obs_across = []
    for d, sent in enumerate(across):
        ring = [(t, (t // quarter ^ 1) * quarter + (t + d) % quarter) for t in range(tiles)]
        obs_across.append(lax.ppermute(sent, "tiles", ring).reshape(slot_count, depth, plane))

    matrices = _matrices(psf_sigma, view_offsets, depth, plane)
    rb_own = _forward(est_bf, matrices[0], matrices[2])
    slots_own = _slots(item_tile, mine * half, half, slot_count)
    held, _ = lax.optimization_barrier((observed[0], matrices[2]))
    (own,) = _pick(held, [half], lambda me, j: me // half * half + j, "pick_own")
    own, rb_own, slots_own, obs_near = lax.optimization_barrier((own, rb_own, slots_own, obs_near))
    obs_own = exchange(own, halves)
    item_tile_other = est_other[blocks * depth :].reshape(-1)[: blocks * views].astype(jnp.int32).reshape(blocks, views)
    slots_other = _slots(item_tile_other, mine * half, half, slot_count, place)
    sent_back = _other(slots_other, est_other, [obs_near, *obs_across], matrices)
    product = lax.ppermute(sent_back, "tiles", swap)
    updated = _own(slots_own, est, obs_own, rb_own, matrices, [product])
    return updated.reshape(blocks, depth, plane)


def solution(mesh):
    return jax.shard_map(
        per_device,
        mesh=mesh,
        in_specs=(
            P(("groups", "tiles"), None, None),
            P(("groups", "tiles"), None, None, None, None),
            P(("groups", "tiles"), None),
            P(),
            P(),
        ),
        out_specs=P(("groups", "tiles"), None, None),
        check_vma=False,
    )
```

```python
import functools

import jax
import jax.numpy as jnp
from jax import lax
from jax.experimental import pallas as pl
from jax.experimental.pallas import tpu as pltpu
from jax.sharding import PartitionSpec as P

BX = 32
BY = 16
TAP_REACH = 15
GROUP = 8
VMEM_LIMIT = 28 << 20
OTHER_COST = pl.CostEstimate(flops=30 * 10**9, transcendentals=0, bytes_accessed=100 << 20)


def _table(sigma, offset, n, transposed):
    i = lax.broadcasted_iota(jnp.int32, (n, n), 1 if transposed else 0)
    k = lax.broadcasted_iota(jnp.int32, (n, n), 0 if transposed else 1)
    half = n // 2
    d = ((k - i - offset + half) & (n - 1)) - half
    df = d.astype(jnp.float32)
    w = jnp.where(jnp.abs(d) <= TAP_REACH, jnp.exp(-df * df / (2.0 * sigma * sigma)), 0.0)
    return (w / jnp.sum(w, axis=0 if transposed else 1, keepdims=True)).astype(jnp.bfloat16)


def _expand(table, size, position):
    n = table.shape[0]
    tall = position(lax.broadcasted_iota(jnp.int32, (size, n), 0)) == lax.broadcasted_iota(jnp.int32, (size, n), 1)
    wide = position(lax.broadcasted_iota(jnp.int32, (n, size), 1)) == lax.broadcasted_iota(jnp.int32, (n, size), 0)
    rows = jnp.dot(tall.astype(jnp.bfloat16), table, preferred_element_type=jnp.float32).astype(jnp.bfloat16)
    return jnp.dot(rows, wide.astype(jnp.bfloat16), preferred_element_type=jnp.float32)


def _matrices_kernel(sigma, offset, wf, wb, zf, zb):
    v = pl.program_id(0)
    depth = zf.shape[-1] // GROUP
    for transposed, w_out, z_out in ((True, wf, zb), (False, wb, zf)):
        z_table = _table(sigma[v, 0], offset[v, 0], depth, transposed)
        y_table = _table(sigma[v, 1], offset[v, 1], BY, transposed)
        x_table = _table(sigma[v, 2], offset[v, 2], BX, transposed)
        plane = BY * BX
        w_out[0] = (
            _expand(y_table, plane, lambda r: r // BX) * _expand(x_table, plane, lambda r: r % BX)
        ).astype(jnp.bfloat16)
        size = GROUP * depth
        r = lax.broadcasted_iota(jnp.int32, (size, size), 0) // depth
        c = lax.broadcasted_iota(jnp.int32, (size, size), 1) // depth
        full = _expand(z_table, size, lambda q: q % depth)
        z_out[0] = jnp.where(r == c, full, 0.0).astype(jnp.bfloat16)


def _matrices(sigma, offset, depth, plane):
    views = sigma.shape[0]
    size = GROUP * depth
    smem = pl.BlockSpec(memory_space=pltpu.SMEM)
    return pl.pallas_call(
        _matrices_kernel,
        grid=(views,),
        in_specs=[smem, smem],
        out_specs=[
            pl.BlockSpec((1, plane, plane), lambda v: (v, 0, 0)),
            pl.BlockSpec((1, plane, plane), lambda v: (v, 0, 0)),
            pl.BlockSpec((1, size, size), lambda v: (v, 0, 0)),
            pl.BlockSpec((1, size, size), lambda v: (v, 0, 0)),
        ],
        out_shape=[
            pltpu.HBM((views, plane, plane), jnp.bfloat16),
            pltpu.HBM((views, plane, plane), jnp.bfloat16),
            jax.ShapeDtypeStruct((views, size, size), jnp.bfloat16),
            jax.ShapeDtypeStruct((views, size, size), jnp.bfloat16),
        ],
        compiler_params=pltpu.CompilerParams(vmem_limit_bytes=VMEM_LIMIT),
        name="matrices",
    )(sigma, offset)


def _forward_kernel(est, wf, zf, rb):
    size = zf.shape[-1]
    p2 = jnp.dot(est[...], wf[0], preferred_element_type=jnp.float32).astype(jnp.bfloat16)
    for g in range(est.shape[0] // size):
        rows = slice(g * size, (g + 1) * size)
        rb[0, rows] = (1.0 / jnp.dot(zf[0], p2[rows], preferred_element_type=jnp.float32)).astype(rb.dtype)


def _forward(est, wf, zf):
    views, plane, _ = wf.shape
    rows, size = est.shape[0], zf.shape[-1]
    return pl.pallas_call(
        _forward_kernel,
        grid=(views,),
        in_specs=[
            pl.BlockSpec((rows, plane), lambda v: (0, 0)),
            pl.BlockSpec((1, plane, plane), lambda v: (v, 0, 0)),
            pl.BlockSpec((1, size, size), lambda v: (v, 0, 0)),
        ],
        out_specs=pl.BlockSpec((1, rows, plane), lambda v: (v, 0, 0)),
        out_shape=pltpu.HBM((views, rows, plane), jnp.bfloat16),
        compiler_params=pltpu.CompilerParams(vmem_limit_bytes=VMEM_LIMIT),
        name="forward",
    )(est, wf, zf)


def _fetch(pairs, sems):
    copies = [pltpu.make_async_copy(src, dst, sems.at[n]) for n, (src, dst) in enumerate(pairs)]
    for copy in copies:
        copy.start()
    return copies


def _spans(total, size):
    return [slice(first, first + size) for first in range(0, total, size)]


def _quotient(slots, obs, v, g):
    return jnp.concatenate([obs[jnp.maximum(slots[v, g * GROUP + j], 0)] for j in range(GROUP)], axis=0)


def _multiply_in(slots, v, acc, correction, depth):
    for b, span in enumerate(_spans(acc.shape[0], depth)):
        acc[span] = acc[span] * jnp.where(slots[v, b] >= 0, correction[span], 1.0)


def _places(arrays, buffer, piece=18):
    out, first = [], 0
    for array in arrays:
        for span in _spans(array.shape[0], piece):
            length = min(span.stop, array.shape[0]) - span.start
            out.append((array.at[pl.ds(span.start, length)], buffer.at[pl.ds(first + span.start, length)]))
        first += array.shape[0]
    return out


def _backward_views(slots, obs, rb, wb, zb, q1, acc, arrive_rb, arrive_wb, finish):
    views, rows, size, depth = rb.shape[0], rb.shape[1], zb.shape[-1], obs.shape[1]
    for v in range(views + 1):
        if v < views:
            arrive_rb(v)
        if v > 0:
            arrive_wb(v - 1)
        if v == views:
            finish()
        if v < views:
            for g, span in enumerate(_spans(rows, size)):
                q = (_quotient(slots, obs, v, g).astype(jnp.float32) * rb[v, span]).astype(jnp.bfloat16)
                q1[v, span] = jnp.dot(zb[v], q, preferred_element_type=jnp.float32).astype(jnp.bfloat16)
        if v > 0:
            correction = jnp.dot(q1[v - 1], wb[v - 1], preferred_element_type=jnp.float32)
            _multiply_in(slots, v - 1, acc, correction, depth)


def _other_kernel(n_obs, n_prior, slots, est, zf, zb, *rest):
    prior, rest = rest[:n_prior], rest[n_prior:]
    wf_hbm, wb_hbm = rest[:2]
    obs_hbm, rest = rest[2 : 2 + n_obs], rest[2 + n_obs :]
    out, wf, wb, obs, p2, rb, acc, sems = rest
    views, size = wf.shape[0], zf.shape[-1]
    pairs = [(wf_hbm.at[v], wf.at[v]) for v in range(views)] + _places(obs_hbm, obs)
    last = len(pairs)
    pairs += [(wb_hbm.at[v], wb.at[v]) for v in range(views)]
    copies = _fetch(pairs, sems)
    acc[...] = prior[0][...].astype(jnp.float32) if n_prior else jnp.ones_like(acc)
    for v in range(views + 1):
        if v < views:
            copies[v].wait()
            p2[v] = jnp.dot(est[: rb.shape[1]], wf[v], preferred_element_type=jnp.float32).astype(jnp.bfloat16)
        if v > 0:
            for span in _spans(rb.shape[1], size):
                rb[v - 1, span] = 1.0 / jnp.dot(zf[v - 1], p2[v - 1, span], preferred_element_type=jnp.float32)
    for copy in copies[views:]:
        copy.wait()
    nothing = lambda *_: None
    _backward_views(slots, obs, rb, wb, zb, p2, acc, nothing, nothing, nothing)
    out[...] = acc[...].astype(out.dtype)


def _own_kernel(n_prior, slots, zb, obs, *rest):
    prior, rest = rest[:n_prior], rest[n_prior:]
    rb_hbm, wb_hbm, est_hbm, acc, rb, wb, est, q1, sems = rest
    views = wb.shape[0]
    pairs = []
    for v in range(views):
        pairs += [(rb_hbm.at[v], rb.at[v]), (wb_hbm.at[v], wb.at[v])]
    copies = _fetch(pairs + [(est_hbm, est)], sems)
    acc[...] = prior[0][...].astype(jnp.float32)

    def finish():
        copies[-1].wait()
        acc[...] = acc[...] * est[...]

    _backward_views(
        slots, obs, rb, wb, zb, q1, acc, lambda v: copies[2 * v].wait(), lambda v: copies[2 * v + 1].wait(), finish
    )


def _call(kernel, name, out_shape, slots, whole, far, obs, near, scratch, cost=None):
    count = sum(o.shape[0] for o in obs)
    smem, vmem, hbm = (pl.BlockSpec(memory_space=m) for m in (pltpu.SMEM, pltpu.VMEM, pltpu.HBM))
    fetched = (*far, *obs, *near)
    n_copies = sum(w.shape[0] for w in far) + sum(len(_spans(o.shape[0], 18)) for o in obs) + len(near)
    return pl.pallas_call(
        kernel,
        in_specs=[smem] + [vmem] * len(whole) + [hbm] * len(fetched),
        out_specs=vmem,
        out_shape=out_shape,
        scratch_shapes=[pltpu.VMEM(w.shape, w.dtype) for w in far]
        + [pltpu.VMEM((count, *o.shape[1:]), o.dtype) for o in obs[:1]]
        + [pltpu.VMEM(w.shape, w.dtype) for w in near]
        + scratch
        + [pltpu.SemaphoreType.DMA((n_copies,))],
        compiler_params=pltpu.CompilerParams(vmem_limit_bytes=VMEM_LIMIT),
        cost_estimate=cost,
        name=name,
    )(slots, *whole, *(pltpu.with_memory_space_constraint(x, pltpu.HBM) for x in fetched))


def _other(slots, est, obs, matrices, prior=()):
    wf, wb, zf, zb = matrices
    rows, plane = slots.shape[1] * obs[0].shape[1], est.shape[1]
    scratch = [
        pltpu.VMEM((wf.shape[0], rows, plane), jnp.bfloat16),
        pltpu.VMEM((wf.shape[0], rows, plane), jnp.float32),
        pltpu.VMEM((rows, plane), jnp.float32),
    ]
    kernel = functools.partial(_other_kernel, len(obs), len(prior))
    out = pltpu.HBM((rows, plane), jnp.bfloat16)
    return _call(kernel, "other", out, slots, (est, zf, zb, *prior), (wf, wb), obs, (), scratch, OTHER_COST)


def _own(slots, est, obs, rb, matrices, prior):
    _, wb, _, zb = matrices
    scratch = [pltpu.VMEM(rb.shape, jnp.bfloat16)]
    kernel = functools.partial(_own_kernel, len(prior))
    out = jax.ShapeDtypeStruct(est.shape, jnp.float32)
    whole = [zb] + [pltpu.with_memory_space_constraint(x, pltpu.VMEM) for x in (obs, *prior)]
    return _call(kernel, "own", out, slots, whole, (rb, wb), (), (est,), scratch)


def _pick_kernel(owners, held, *rest):
    *outs, buffer, sems_in, sems_out = rest
    me = lax.axis_index("tiles")
    half = buffer.shape[0]
    copies = _fetch([(held.at[owners(me, j)], buffer.at[j]) for j in range(half)], sems_in)
    back, places = [], [out.at[n] for out in outs for n in range(out.shape[0])]
    for j in range(half):
        copies[j].wait()
        back.append(pltpu.make_async_copy(buffer.at[j], places[j], sems_out.at[j]))
        back[j].start()
    for copy in back:
        copy.wait()


def _pick(held, counts, owners, name):
    hbm = pl.BlockSpec(memory_space=pltpu.HBM)
    half = sum(counts)
    return pl.pallas_call(
        functools.partial(_pick_kernel, owners),
        in_specs=[hbm],
        out_specs=[hbm] * len(counts),
        out_shape=[pltpu.HBM((count, *held.shape[1:]), held.dtype) for count in counts],
        scratch_shapes=[
            pltpu.VMEM((half, *held.shape[1:]), held.dtype),
            pltpu.SemaphoreType.DMA((half,)),
            pltpu.SemaphoreType.DMA((half,)),
        ],
        name=name,
    )(held)


def _slots(item_tile, first, count, slot_count, place=lambda tile: tile):
    blocks, views = item_tile.shape
    flat = item_tile.reshape(-1)
    order = jnp.arange(blocks * views, dtype=jnp.int32)
    before = (flat[:, None] == flat[None, :]) & (order[None, :] < order[:, None])
    rank = jnp.sum(before.astype(jnp.int32), axis=1)
    tile = flat - first
    slot = jnp.where((tile >= 0) & (tile < count), place(tile) * slot_count + rank, -1)
    return slot.reshape(blocks, views).T


def per_device(estimate, observed, item_tile, psf_sigma, view_offsets):
    blocks, depth, plane = estimate.shape
    tiles, slot_count = observed.shape[1:3]
    views = item_tile.shape[1]
    half, quarter = tiles // 2, tiles // 4
    me = lax.axis_index("tiles")
    mine, side, turn = me // half, me // quarter % 2, me % quarter
    halves = [list(range(first, first + half)) for first in range(0, tiles, half)]
    quarters = [list(range(first, first + quarter)) for first in range(0, tiles, quarter)]
    swap = [(t, (t + half) % tiles) for t in range(tiles)]

    def exchange(sent, groups):
        got = lax.all_to_all(sent, "tiles", 0, 0, axis_index_groups=groups, tiled=True)
        return got.reshape(-1, depth, plane)

    def owner(me, j):
        near = me // quarter % 2 * quarter + j
        across = (1 - me // quarter % 2) * quarter + (me + j) % quarter
        return (1 - me // half) * half + (near if j < quarter else across)

    def place(tile):
        return jnp.where(tile // quarter == side, tile % quarter, quarter + (turn - tile % quarter + quarter) % quarter)

    est = estimate.reshape(blocks * depth, plane)
    est_bf = est.astype(jnp.bfloat16)
    names = item_tile.reshape(-1).astype(jnp.bfloat16)
    names = jnp.pad(names, (0, depth * plane - names.shape[0])).reshape(depth, plane)
    est_other = lax.ppermute(jnp.concatenate([est_bf, names], axis=0), "tiles", swap)
    near, *across = _pick(observed[0], [quarter] + [1] * quarter, owner, "pick_other")
    obs_near = exchange(near, quarters)
    obs_across = []
    for d, sent in enumerate(across):
        ring = [(t, (t // quarter ^ 1) * quarter + (t + d) % quarter) for t in range(tiles)]
        obs_across.append(lax.ppermute(sent, "tiles", ring).reshape(slot_count, depth, plane))

    matrices = _matrices(psf_sigma, view_offsets, depth, plane)
    rb_own = _forward(est_bf, matrices[0], matrices[2])
    slots_own = _slots(item_tile, mine * half, half, slot_count)
    held, obs_near = lax.optimization_barrier((observed[0], obs_near))
    (own,) = _pick(held, [half], lambda me, j: me // half * half + j, "pick_own")
    obs_own = exchange(own, halves)
    item_tile_other = est_other[blocks * depth :].reshape(-1)[: blocks * views].astype(jnp.int32).reshape(blocks, views)
    slots_other = _slots(item_tile_other, mine * half, half, slot_count, place)
    sent_back = _other(slots_other, est_other, [obs_near, *obs_across], matrices)
    product = lax.ppermute(sent_back, "tiles", swap)
    updated = _own(slots_own, est, obs_own, rb_own, matrices, [product])
    return updated.reshape(blocks, depth, plane)


def solution(mesh):
    return jax.shard_map(
        per_device,
        mesh=mesh,
        in_specs=(
            P(("groups", "tiles"), None, None),
            P(("groups", "tiles"), None, None, None, None),
            P(("groups", "tiles"), None),
            P(),
            P(),
        ),
        out_specs=P(("groups", "tiles"), None, None),
        check_vma=False,
    )
```
